32 devices in a mesh: dp: 4 (over x, core), expert: 8 (over z, y).
Axes of the slice: x: 2, y: 2, z: 4, core: 2. Of those that a mesh axis runs over, the one named last changes fastest.
Arguments:
- tokens: bfloat16 [2048, 4096], P('expert'), may hold values from -6 to 6
- expert_ids: int32 [2048, 8], P('expert'), may hold values from 0 to 255, as said below
- combine_weight: float32 [2048, 8], P('expert'), may hold values from 0.1 to 1
- old_plan: int32 [8], replicated, may hold values from 0 to 255, as said below
- new_plan: int32 [8], replicated, may hold values from 0 to 255, as said below
- gate_weight: bfloat16 [8, 4096, 2048], P('expert', None, 'dp'), may hold values from -0.09375 to 0.09375
- up_weight: bfloat16 [8, 4096, 2048], P('expert', None, 'dp'), may hold values from -0.09375 to 0.09375
- down_weight: bfloat16 [8, 2048, 4096], P('expert', 'dp'), may hold values from -0.125 to 0.125
- shared_gate: bfloat16 [4096, 2048], P(None, 'dp'), may hold values from -0.09375 to 0.09375
- shared_up: bfloat16 [4096, 2048], P(None, 'dp'), may hold values from -0.09375 to 0.09375
- shared_down: bfloat16 [2048, 4096], P('dp'), may hold values from -0.125 to 0.125
Outputs:
- mixed_out: bfloat16 [2048, 4096], P('expert', 'dp')
The draws below stay inside these ranges and needn't reach their ends.
Inputs may be any that keep to these rules, and one draw needn't show every extreme that they name: `old_plan`: the 8 experts are different. `new_plan`: slot s holds old_plan[s] or old_plan[s - 1] (slot 0 may take from slot 7); slots 0, 4 and 7 change; apart from slots 0 and 7, two neighbouring slots never both change. `expert_ids`: the 8 experts of a token are different; the tokens of one device send at most 2 kept routes to the slots of one expert together, and some slot gets exactly 2 from the tokens of every device.
All inputs are finite; a program needn't handle non-finite values.
Results may differ from the reference program's by a relative error of at most 0.014.
Values may be sent and summed in bfloat16 or wider, within the bound.
No kernel may reach another device: no remote copies, remote signals or barrier semaphores. Data moves between devices by JAX's collectives and lax.ppermute only.
A program may use at most 64 MiB of HBM per device.

```python
import jax
import jax.numpy as jnp
from jax import lax

D = 4096
H = 2048
EXPERTS = 256
TOPK = 8
CAP = 2
TOK_DEV = 256
SLOTS = 8
TOKENS = 2048
N_DP = 4


def plans_of(key):
    shuffled = jax.random.permutation(jax.random.fold_in(key, 101), EXPERTS)
    older = shuffled[:SLOTS].astype(jnp.int32)
    places = jnp.arange(SLOTS)
    middle = SLOTS // 2
    inner = (places >= 2) & (places <= SLOTS - 3)
    inner = inner & (places != middle - 1) & (places != middle) & (places != middle + 1)
    marks = (jax.random.randint(jax.random.fold_in(key, 102), (SLOTS,), 0, 4) == 0) & inner
    changed = marks & jnp.logical_not(jnp.roll(marks, 1))
    changed = changed | (places == 0) | (places == SLOTS - 1) | (places == middle)
    newer = jnp.where(changed, jnp.roll(older, 1), older).astype(jnp.int32)
    return (older, newer)


def routing_of(key):
    older, newer = plans_of(key)
    slot_row = jnp.arange(SLOTS)
    same_slot = newer[:, None] == newer[None, :]
    slot_rank = jnp.sum((same_slot & (slot_row[None, :] < slot_row[:, None])).astype(jnp.int32), axis=1)
    slot_copies = jnp.sum(same_slot.astype(jnp.int32), axis=1)
    counts = jax.random.randint(jax.random.fold_in(key, 201), (SLOTS, SLOTS), 0, CAP + 1)
    counts = jnp.where((slot_rank > 0)[None, :], 0, counts)
    fill_scores = jax.random.randint(jax.random.fold_in(key, 202), (SLOTS,), 0, 1 << 20)
    filled = jnp.argmax(jnp.where(slot_copies == 1, fill_scores, -1))
    counts = jnp.where(slot_row[None, :] == filled, CAP, counts)
    ends = jnp.cumsum(counts, axis=1)
    entries = jnp.arange(TOK_DEV)
    listed = jnp.sum((ends[:, None, :] <= entries[None, :, None]).astype(jnp.int32), axis=2)
    device_keys = jax.random.split(jax.random.fold_in(key, 203), SLOTS)
    shuffles = jax.vmap(lambda one_key: jax.random.permutation(one_key, TOK_DEV))(device_keys)
    slot_token = jnp.take_along_axis(listed, shuffles, axis=1)
    resident = slot_token < SLOTS
    safe_slot = jnp.minimum(slot_token, SLOTS - 1)
    expert_here = newer[safe_slot]
    in_plan = jnp.sum((newer[:, None] == jnp.arange(EXPERTS)[None, :]).astype(jnp.int32), axis=0) > 0
    scores = jax.random.randint(jax.random.fold_in(key, 204), (SLOTS, TOK_DEV, EXPERTS), 0, 1 << 20) * EXPERTS + jnp.arange(EXPERTS)[None, None, :]
    scores = jnp.where(in_plan[None, None, :], -1, scores)
    others = lax.top_k(scores, TOPK)[1].astype(jnp.int32)
    spot = jax.random.randint(jax.random.fold_in(key, 205), (SLOTS, TOK_DEV), 0, TOPK)
    at_spot = (jnp.arange(TOPK)[None, None, :] == spot[:, :, None]) & resident[:, :, None]
    chosen_ids = jnp.where(at_spot, expert_here[:, :, None], others).astype(jnp.int32)
    return chosen_ids.reshape(TOKENS, TOPK)


def draw_old_plan(key, part):
    return plans_of(key)[0]


def draw_new_plan(key, part):
    return plans_of(key)[1]


def draw_expert_ids(key, part):
    return routing_of(key)


def block_levels(own_key, shape, shards, smallest, high):
    def one(axis_at, blocks):
        draws = jax.random.uniform(jax.random.fold_in(jax.random.fold_in(own_key, 6), axis_at), (blocks,), jnp.float32, smallest / len(shards), high / len(shards))
        return jnp.repeat(jnp.exp(draws), shape[axis_at] // blocks).reshape((-1,) + (1,) * (len(shape) - axis_at - 1))

    loudness = one(*shards[0])
    for cut in shards[1:]:
        loudness = loudness * one(*cut)
    return loudness


def centred(rng, dims, scale, reach, shards=(), held_as=jnp.bfloat16):
    result = scale * jax.random.normal(rng, dims, jnp.float32)
    if shards:
        result = result * block_levels(rng, dims, shards, -0.22, 0.18)
    return jnp.clip(result, -reach, reach).astype(held_as)


def setup_inputs(seed: int = 0) -> dict:
    seeds = jax.random.split(jax.random.key(seed), 12)
    tokens = centred(seeds[0], (TOKENS, D), 1.0, 6.0, ((0, 8),))
    expert_ids = draw_expert_ids(jax.random.fold_in(seeds[11], 71), 0)
    combine_weight = jnp.clip(0.1 + 0.9 * jax.random.uniform(seeds[2], (TOKENS, TOPK), jnp.float32) ** block_levels(seeds[2], (TOKENS, TOPK), ((0, 8),), -0.2, 0.2), 0.1, 1.0)
    old_plan = draw_old_plan(jax.random.fold_in(seeds[11], 71), 0)
    new_plan = draw_new_plan(jax.random.fold_in(seeds[11], 71), 0)
    gate_weight = centred(seeds[5], (SLOTS, D, H), D ** -0.5, 0.09375, ((0, 8), (2, 4)))
    up_weight = centred(seeds[6], (SLOTS, D, H), D ** -0.5, 0.09375, ((0, 8), (2, 4)))
    down_weight = centred(seeds[7], (SLOTS, H, D), H ** -0.5, 0.125, ((0, 8), (1, 4)))
    shared_gate = centred(seeds[8], (D, H), D ** -0.5, 0.09375, ((1, 4),))
    shared_up = centred(seeds[9], (D, H), D ** -0.5, 0.09375, ((1, 4),))
    shared_down = centred(seeds[10], (H, D), H ** -0.5, 0.125, ((0, 4),))
    return dict(tokens=tokens, expert_ids=expert_ids, combine_weight=combine_weight, old_plan=old_plan, new_plan=new_plan, gate_weight=gate_weight, up_weight=up_weight, down_weight=down_weight, shared_gate=shared_gate, shared_up=shared_up, shared_down=shared_down)


def route_slots(expert_ids, token_index, new_plan):
    matches = (expert_ids[:, :, None] == new_plan[None, None, :]).astype(jnp.int32)
    counted = jnp.sum(matches, axis=2, keepdims=True)
    before = jnp.cumsum(matches, axis=2) - matches
    wanted = jnp.remainder(token_index[:, None, None], jnp.maximum(counted, 1))
    return matches * (before == wanted).astype(jnp.int32)


def silu_product(row_block, gate_full, up_full):
    gate_value = jnp.dot(row_block, gate_full, preferred_element_type=jnp.float32)
    up_value = jnp.dot(row_block, up_full, preferred_element_type=jnp.float32)
    return (jax.nn.silu(gate_value) * up_value).astype(jnp.bfloat16)


def blocked_expert(row_block, gate_full, up_full, down_full):
    hidden = silu_product(row_block, gate_full, up_full)
    width_block = H // N_DP
    summed = jnp.zeros((row_block.shape[0], down_full.shape[1]), jnp.float32)
    for block_index in range(N_DP):
        offset = block_index * width_block
        partial_value = jnp.dot(hidden[:, offset:offset + width_block], down_full[offset:offset + width_block], preferred_element_type=jnp.float32).astype(jnp.bfloat16)
        partial_value = lax.optimization_barrier(partial_value)
        summed = summed + partial_value.astype(jnp.float32)
    return summed


def reference(tokens, expert_ids, combine_weight, old_plan, new_plan, gate_weight, up_weight, down_weight, shared_gate, shared_up, shared_down):
    token_index = jnp.arange(TOKENS, dtype=jnp.int32)
    chosen = route_slots(expert_ids, token_index, new_plan)
    slot_index = jnp.arange(SLOTS, dtype=jnp.int32)
    present = jnp.sum(chosen, axis=2)
    target = jnp.sum(chosen * slot_index[None, None, :], axis=2)
    flat_slot = jnp.where(present > 0, target, SLOTS).reshape(-1).astype(jnp.int32)
    flat_weight = combine_weight.reshape(-1)
    changed = (new_plan != old_plan).astype(jnp.int32)
    source = jnp.remainder(slot_index - changed, SLOTS).astype(jnp.int32)
    limit = CAP * SLOTS

    def one_slot(slot):
        found = jnp.nonzero(flat_slot == slot, size=limit, fill_value=0)[0].astype(jnp.int32)
        valid = (flat_slot[found] == slot).astype(jnp.float32)
        owner = (found // TOPK).astype(jnp.int32)
        row_block = tokens[owner]
        anchor = source[slot]
        output = blocked_expert(row_block, gate_weight[anchor], up_weight[anchor], down_weight[anchor])
        return owner, output * (flat_weight[found] * valid)[:, None]

    owners, contribution = lax.map(one_slot, slot_index)
    routed = jnp.zeros((TOKENS, D), jnp.float32).at[owners.reshape(-1)].add(contribution.reshape(-1, D))
    shared = blocked_expert(tokens, shared_gate, shared_up, shared_down)
    return (shared + routed).astype(jnp.bfloat16)
```

```python
import functools

import jax
import jax.numpy as jnp
from jax import lax
from jax.experimental import pallas as pl
from jax.experimental.pallas import tpu as pltpu
from jax.sharding import PartitionSpec as P

CAP = 2
BF = jnp.bfloat16
F32 = jnp.float32
VMEM = pltpu.VMEM
ANY = pl.ANY
SMEM = pltpu.SMEM


def silu_mul(gate_value, up_value):
    return (gate_value / (1.0 + jnp.exp(-gate_value)) * up_value).astype(BF)


def dot(a, b):
    return jnp.dot(a, b, preferred_element_type=F32)


def route_rows(ids, weight, old_ref, new_ref, rows, slots, slot_of_row, rank_of_row):
    tok = ids.shape[1]
    plan = jnp.full((rows, 1), -1, jnp.int32)
    for slot in range(slots):
        expert = old_ref[slot]
        after = (slot + 1) % slots
        present = (new_ref[slot] == expert) | (new_ref[after] == expert)
        plan = jnp.where(slot_of_row == slot, jnp.where(present, expert, -1), plan)
    hit = jnp.zeros((rows, tok), F32)
    scale = jnp.zeros((rows, tok), F32)
    for k in range(ids.shape[0]):
        same = ids[k : k + 1, :] == plan
        hit = jnp.where(same, 1.0, hit)
        if weight is not None:
            scale = jnp.where(same, weight[k : k + 1, :], scale)
    earlier = lax.broadcasted_iota(jnp.int32, (tok, tok), 0)
    later = lax.broadcasted_iota(jnp.int32, (tok, tok), 1)
    before = dot(hit.astype(BF), jnp.where(earlier < later, 1.0, 0.0).astype(BF))
    chosen = jnp.where(before == rank_of_row.astype(F32), hit, 0.0)
    return chosen, scale


def dispatch_kernel(slots, old_ref, new_ref, ids_ref, tok_ref, out_ref):
    rows = slots * CAP
    row = lax.broadcasted_iota(jnp.int32, (rows, 1), 0)
    chosen, _ = route_rows(
        ids_ref[...], None, old_ref, new_ref, rows, slots, row // CAP, row % CAP
    )
    picked = dot(chosen.astype(BF), tok_ref[...]).astype(BF)
    for slot in range(slots):
        out_ref[slot] = picked[slot * CAP : (slot + 1) * CAP, :]


def combine_kernel(
    slots, parts, old_ref, new_ref, ids_ref, weight_ref, back_ref, *rest
):
    sums, (out_ref, rows_ref) = rest[:-2], rest[-2:]
    rows = slots * parts * CAP
    row = lax.broadcasted_iota(jnp.int32, (rows, 1), 0)
    chosen, scale = route_rows(
        ids_ref[...],
        weight_ref[...],
        old_ref,
        new_ref,
        rows,
        slots,
        row // (parts * CAP),
        row % CAP,
    )
    mix = chosen * scale
    high = mix.astype(BF)
    low = (mix - high.astype(F32)).astype(BF)
    for block in range(slots * parts):
        rows_ref[block * CAP : (block + 1) * CAP, :] = back_ref[block]
    dims = (((0,), (0,)), ((), ()))
    total = lax.dot_general(high, rows_ref[...], dims, preferred_element_type=F32)
    total = total + lax.dot_general(low, rows_ref[...], dims, preferred_element_type=F32)
    for term in sums:
        total = total + term[...].astype(F32)
    out_ref[...] = total.astype(BF)


def shared_first_kernel(
    chips,
    steps,
    place_ref,
    tok_ref,
    gate_ref,
    up_ref,
    down_ref,
    send_ref,
    keep_ref,
    hidden_ref,
    gate_buf,
    up_buf,
    down_buf,
    gate_acc,
    up_acc,
    gate_sem,
    up_sem,
    down_sem,
):
    depth = gate_ref.shape[0] // steps
    width = send_ref.shape[2]
    gates, ups, downs = [], [], []
    for step in range(steps):
        part = pl.ds(step * depth, depth)
        gates.append(
            pltpu.make_async_copy(gate_ref.at[part], gate_buf.at[part], gate_sem.at[step])
        )
        ups.append(pltpu.make_async_copy(up_ref.at[part], up_buf.at[part], up_sem.at[step]))
    for block in range(2 * (chips - 1)):
        columns = pl.ds(pl.multiple_of(place_ref[block] * width, width), width)
        downs.append(
            pltpu.make_async_copy(
                down_ref.at[:, columns], down_buf.at[block], down_sem.at[block]
            )
        )
    for copy in [c for pair in zip(gates, ups) for c in pair] + downs:
        copy.start()
    for step in range(steps):
        part = pl.ds(step * depth, depth)
        gates[step].wait()
        ups[step].wait()
        rows = tok_ref[:, part]
        gate_value = dot(rows, gate_buf[part, :])
        up_value = dot(rows, up_buf[part, :])
        if step:
            gate_value = gate_value + gate_acc[...]
            up_value = up_value + up_acc[...]
        if step < steps - 1:
            gate_acc[...] = gate_value
            up_acc[...] = up_value
        else:
            hidden_ref[...] = silu_mul(gate_value, up_value)
    for block in range(2 * (chips - 1)):
        downs[block].wait()
        target = send_ref if block % 2 == 0 else keep_ref
        target[block // 2] = dot(hidden_ref[...], down_buf[block]).astype(BF)


def shared_rest_kernel(place_ref, hidden_ref, down_ref, send_ref, keep_ref, down_buf, down_sem):
    width = send_ref.shape[1]
    downs = []
    for block in range(2):
        columns = pl.ds(pl.multiple_of(place_ref[block] * width, width), width)
        downs.append(
            pltpu.make_async_copy(
                down_ref.at[:, columns], down_buf.at[block], down_sem.at[block]
            )
        )
        downs[-1].start()
    for block, target in enumerate((send_ref, keep_ref)):
        downs[block].wait()
        target[...] = dot(hidden_ref[...], down_buf[block]).astype(BF)


def routed_kernel(
    steps,
    parts,
    in_ref,
    gate_ref,
    up_ref,
    down_ref,
    out_ref,
    rows_ref,
    gate_buf,
    up_buf,
    down_buf,
    gate_sem,
    up_sem,
    down_sem,
):
    depth = gate_ref.shape[1] // steps
    senders = in_ref.shape[0]
    width = out_ref.shape[2]
    gates, ups, downs = [], [], []
    for step in range(steps):
        part = pl.ds(step * depth, depth)
        gates.append(
            pltpu.make_async_copy(gate_ref.at[0, part], gate_buf.at[part], gate_sem.at[step])
        )
        ups.append(pltpu.make_async_copy(up_ref.at[0, part], up_buf.at[part], up_sem.at[step]))
    for part in range(parts):
        columns = pl.ds(part * width, width)
        downs.append(
            pltpu.make_async_copy(
                down_ref.at[0, :, columns], down_buf.at[part], down_sem.at[part]
            )
        )
    for copy in [c for pair in zip(gates, ups) for c in pair] + downs:
        copy.start()
    for sender in range(senders):
        rows_ref[sender * CAP : (sender + 1) * CAP, :] = in_ref[sender]
    gate_value = up_value = 0.0
    for step in range(steps):
        part = pl.ds(step * depth, depth)
        gates[step].wait()
        ups[step].wait()
        rows = rows_ref[:, part]
        gate_value = gate_value + dot(rows, gate_buf[part, :])
        up_value = up_value + dot(rows, up_buf[part, :])
    hidden = silu_mul(gate_value, up_value)
    for part in range(parts):
        downs[part].wait()
        value = dot(hidden, down_buf[part]).astype(BF)
        for sender in range(senders):
            out_ref[sender * parts + part] = value[sender * CAP : (sender + 1) * CAP, :]


def spec(space):
    return pl.BlockSpec(memory_space=space)


def local(
    tokens,
    expert_ids,
    combine_weight,
    old_plan,
    new_plan,
    gate_weight,
    up_weight,
    down_weight,
    shared_gate,
    shared_up,
    shared_down,
):
    slots = lax.axis_size("expert")
    parts = lax.axis_size("dp")
    chips = parts // 2
    tok, model = tokens.shape
    hidden_width = shared_gate.shape[1]
    width = model // parts
    steps = 8
    me = lax.axis_index("dp")
    chip, core = me // 2, me % 2
    ids = expert_ids.T
    weight = combine_weight.T
    dma = pltpu.SemaphoreType.DMA

    outgoing = pl.pallas_call(
        functools.partial(dispatch_kernel, slots),
        out_shape=jax.ShapeDtypeStruct((slots, CAP, model), BF),
        in_specs=[spec(SMEM), spec(SMEM), spec(VMEM), spec(VMEM)],
        out_specs=spec(VMEM),
        name="dispatch",
    )(old_plan, new_plan, ids, tokens)
    arrived = lax.all_to_all(outgoing, "expert", split_axis=0, concat_axis=0, tiled=True)

    others = [(chip + k) % chips for k in range(1, chips)]
    place_first = jnp.stack([q * 2 + b for q in others for b in (1 - core, core)])
    place_rest = jnp.stack([chip * 2 + 1 - core, chip * 2 + core])
    send, keep, hidden = pl.pallas_call(
        functools.partial(shared_first_kernel, chips, steps),
        out_shape=(
            jax.ShapeDtypeStruct((chips - 1, tok, width), BF),
            jax.ShapeDtypeStruct((chips - 1, tok, width), BF),
            jax.ShapeDtypeStruct((tok, hidden_width), BF),
        ),
        in_specs=[spec(SMEM), spec(VMEM), spec(ANY), spec(ANY), spec(ANY)],
        out_specs=(spec(VMEM),) * 3,
        scratch_shapes=[
            VMEM((model, hidden_width), BF),
            VMEM((model, hidden_width), BF),
            VMEM((2 * (chips - 1), hidden_width, width), BF),
            VMEM((tok, hidden_width), F32),
            VMEM((tok, hidden_width), F32),
            dma((steps,)),
            dma((steps,)),
            dma((2 * (chips - 1),)),
        ],
        name="shared_first",
        cost_estimate=pl.CostEstimate(
            flops=4 * tok * model * hidden_width + 2 * tok * hidden_width * model // 2,
            bytes_accessed=5 * model * hidden_width,
            transcendentals=0,
        ),
    )(place_first, tokens, shared_gate, shared_up, shared_down)

    pairs = [(j, j ^ 1) for j in range(parts)]
    partner = lax.ppermute(send, "dp", pairs)
    chip_sum = (partner.astype(F32) + keep.astype(F32)).astype(BF)
    sums = []
    for k in range(1, chips):
        moves = [(j, (j // 2 + k) % chips * 2 + j % 2) for j in range(parts)]
        sums.append(lax.ppermute(chip_sum[k - 1], "dp", moves))

    send_rest, keep_rest = pl.pallas_call(
        shared_rest_kernel,
        out_shape=(jax.ShapeDtypeStruct((tok, width), BF),) * 2,
        in_specs=[spec(SMEM), spec(VMEM), spec(ANY)],
        out_specs=(spec(VMEM),) * 2,
        scratch_shapes=[VMEM((2, hidden_width, width), BF), dma((2,))],
        name="shared_rest",
        cost_estimate=pl.CostEstimate(
            flops=4 * tok * hidden_width * width,
            bytes_accessed=4 * hidden_width * width,
            transcendentals=0,
        ),
    )(place_rest, hidden, shared_down)
    sums += [keep_rest, lax.ppermute(send_rest, "dp", pairs)]

    routed = pl.pallas_call(
        functools.partial(routed_kernel, steps, parts),
        out_shape=jax.ShapeDtypeStruct((slots * parts, CAP, width), BF),
        in_specs=[spec(VMEM), spec(ANY), spec(ANY), spec(ANY)],
        out_specs=spec(VMEM),
        scratch_shapes=[
            VMEM((slots * CAP, model), BF),
            VMEM((model, hidden_width), BF),
            VMEM((model, hidden_width), BF),
            VMEM((parts, hidden_width, width), BF),
            dma((steps,)),
            dma((steps,)),
            dma((parts,)),
        ],
        name="routed",
        cost_estimate=pl.CostEstimate(
            flops=6 * tok * model * hidden_width,
            bytes_accessed=6 * model * hidden_width,
            transcendentals=0,
        ),
    )(arrived, gate_weight, up_weight, down_weight)
    back = lax.all_to_all(routed, ("expert", "dp"), split_axis=0, concat_axis=0, tiled=True)

    return pl.pallas_call(
        functools.partial(combine_kernel, slots, parts),
        out_shape=jax.ShapeDtypeStruct((tok, width), BF),
        in_specs=[spec(SMEM), spec(SMEM)] + [spec(VMEM)] * (3 + len(sums)),
        out_specs=spec(VMEM),
        scratch_shapes=[VMEM((slots * parts * CAP, width), BF)],
        name="combine",
    )(old_plan, new_plan, ids, weight, back, *sums)


def solution(mesh):
    in_specs = (
        P("expert", None),
        P("expert", None),
        P("expert", None),
        P(),
        P(),
        P("expert", None, "dp"),
        P("expert", None, "dp"),
        P("expert", "dp", None),
        P(None, "dp"),
        P(None, "dp"),
        P("dp", None),
    )
    out_specs = P("expert", "dp")
    return jax.shard_map(local, mesh=mesh, in_specs=in_specs, out_specs=out_specs, check_vma=False)
```

```python
import functools

import jax
import jax.numpy as jnp
from jax import lax
from jax.experimental import pallas as pl
from jax.experimental.pallas import tpu as pltpu
from jax.sharding import PartitionSpec as P


CAP = 2
BF = jnp.bfloat16
F32 = jnp.float32
VMEM = pltpu.VMEM
ANY = pl.ANY
SMEM = pltpu.SMEM


def silu_mul(gate_value, up_value):
    return (gate_value / (1.0 + jnp.exp(-gate_value)) * up_value).astype(BF)


def dot(a, b):
    return jnp.dot(a, b, preferred_element_type=F32)


def route_rows(ids, weight, old_ref, new_ref, slot_of, span, slots, ranks):
    tok = ids.shape[1]
    rows = slots * span * ranks
    row = lax.broadcasted_iota(jnp.int32, (rows, 1), 0)
    block, rank = row // (span * ranks), row % ranks
    plan = jnp.full((rows, 1), -1, jnp.int32)
    for index in range(slots):
        slot = slot_of(index)
        expert = old_ref[slot]
        present = (new_ref[slot] == expert) | (new_ref[lax.rem(slot + 1, slots)] == expert)
        plan = jnp.where(block == index, jnp.where(present, expert, -1), plan)
    hit = jnp.zeros((rows, tok), F32)
    scale = jnp.zeros((rows, tok), F32)
    for k in range(ids.shape[0]):
        same = ids[k : k + 1, :] == plan
        hit = jnp.where(same, 1.0, hit)
        if weight is not None:
            scale = jnp.where(same, weight[k : k + 1, :], scale)
    earlier = lax.broadcasted_iota(jnp.int32, (tok, tok), 0)
    later = lax.broadcasted_iota(jnp.int32, (tok, tok), 1)
    before = dot(hit.astype(BF), jnp.where(earlier < later, 1.0, 0.0).astype(BF))
    chosen = jnp.where(before == rank.astype(F32), hit, 0.0)
    return chosen, scale


def ready_kernel(out_ref):
    out_ref[...] = jnp.zeros_like(out_ref)


def select_kernel(slots, old_ref, new_ref, ids_ref, after_ref, chosen_ref):
    me = lax.axis_index("expert")
    chosen, _ = route_rows(
        ids_ref[...], None, old_ref, new_ref, lambda k: me ^ k, 1, slots, CAP
    )
    chosen_ref[...] = chosen.astype(BF)


def pick_kernel(slots, chosen_ref, tok_ref, own_ref, send_ref):
    picked = dot(chosen_ref[...], tok_ref[...]).astype(BF)
    half = slots // 2
    for k in range(slots):
        target = own_ref if k < half else send_ref
        target[k % half] = picked[k * CAP : (k + 1) * CAP, :]


def pack_kernel(places, *refs):
    for target, (array, index) in enumerate(places):
        refs[-1][target] = refs[array][index]


def add_kernel(a_ref, b_ref, out_ref):
    out_ref[...] = (a_ref[...].astype(F32) + b_ref[...].astype(F32)).astype(BF)


def mix_kernel(slots, parts, old_ref, new_ref, ids_ref, weight_ref, after_ref, high_ref, low_ref):
    chosen, scale = route_rows(
        ids_ref[...], weight_ref[...], old_ref, new_ref, lambda k: k, parts, slots, CAP
    )
    mix = chosen * scale
    high = mix.astype(BF)
    high_ref[...] = high
    low_ref[...] = (mix - high.astype(F32)).astype(BF)


def combine_kernel(blocks, high_ref, low_ref, back_ref, *rest):
    sums, (out_ref, rows_ref) = rest[:-2], rest[-2:]
    for block in range(blocks):
        rows_ref[block * CAP : (block + 1) * CAP, :] = back_ref[block]
    dims = (((0,), (0,)), ((), ()))
    total = lax.dot_general(high_ref[...], rows_ref[...], dims, preferred_element_type=F32)
    total = total + lax.dot_general(low_ref[...], rows_ref[...], dims, preferred_element_type=F32)
    for term in sums:
        total = total + term[...].astype(F32)
    out_ref[...] = total.astype(BF)


def column_block(chip, core, width):
    return pl.ds(pl.multiple_of((chip * 2 + core) * width, width), width)


def shared_first_kernel(
    chips, tok_ref, gate_ref, up_ref, down_ref, after_ref, send_ref, keep_ref, hidden_ref
):
    width = send_ref.shape[2]
    me = lax.axis_index("dp")
    chip, core = me // 2, me % 2
    hidden_ref[...] = silu_mul(dot(tok_ref[...], gate_ref[...]), dot(tok_ref[...], up_ref[...]))
    for k in range(1, chips):
        other = lax.rem(chip + k, chips)
        for target, side in ((send_ref, 1 - core), (keep_ref, core)):
            block = down_ref[:, column_block(other, side, width)]
            target[k - 1] = dot(hidden_ref[...], block).astype(BF)


def shared_rest_kernel(hidden_ref, down_ref, after_ref, send_ref, keep_ref):
    width = send_ref.shape[1]
    me = lax.axis_index("dp")
    chip, core = me // 2, me % 2
    for target, side in ((send_ref, 1 - core), (keep_ref, core)):
        block = down_ref[:, column_block(chip, side, width)]
        target[...] = dot(hidden_ref[...], block).astype(BF)


def routed_kernel(parts, places, *refs):
    arrays, (gate_ref, up_ref, down_ref, out_ref, rows_ref) = refs[:-5], refs[-5:]
    width = out_ref.shape[2]
    me = lax.axis_index("expert")
    for k, (array, index) in enumerate(places):
        rows_ref[k * CAP : (k + 1) * CAP, :] = arrays[array][index]
    rows = rows_ref[...]
    hidden = silu_mul(dot(rows, gate_ref[0]), dot(rows, up_ref[0]))
    for part in range(parts):
        value = dot(hidden, down_ref[0, :, part * width : (part + 1) * width]).astype(BF)
        for k in range(len(places)):
            out_ref[(me ^ k) * parts + part] = value[k * CAP : (k + 1) * CAP, :]


def cost(flops, size):
    return pl.CostEstimate(flops=flops, bytes_accessed=size, transcendentals=0)


def params(megabytes):
    return pltpu.CompilerParams(vmem_limit_bytes=megabytes * 1024 * 1024)


def spec(space):
    return pl.BlockSpec(memory_space=space)


def local(
    tokens,
    expert_ids,
    combine_weight,
    old_plan,
    new_plan,
    gate_weight,
    up_weight,
    down_weight,
    shared_gate,
    shared_up,
    shared_down,
):
    slots = lax.axis_size("expert")
    parts = lax.axis_size("dp")
    chips = parts // 2
    tok, model = tokens.shape
    hidden_width = shared_gate.shape[1]
    width = model // parts
    ids = expert_ids.T
    weight = combine_weight.T
    rows = jax.ShapeDtypeStruct((tok, width), BF)

    half = slots // 2
    blocks = jax.ShapeDtypeStruct((half, CAP, model), BF)
    ready = pl.pallas_call(
        ready_kernel,
        out_shape=jax.ShapeDtypeStruct((8, 128), F32),
        out_specs=spec(VMEM),
        name="ready",
        cost_estimate=cost(20 * tok * model * hidden_width, 0),
        compiler_params=params(1),
    )()
    chosen = pl.pallas_call(
        functools.partial(select_kernel, slots),
        out_shape=jax.ShapeDtypeStruct((slots * CAP, tok), BF),
        in_specs=[spec(SMEM), spec(SMEM), spec(VMEM), spec(ANY)],
        out_specs=spec(VMEM),
        name="select",
        cost_estimate=cost(2 * slots * CAP * tok * tok, 2 * tok * model),
        compiler_params=params(2),
    )(old_plan, new_plan, ids, ready)
    own, moving = pl.pallas_call(
        functools.partial(pick_kernel, slots),
        out_shape=(blocks, blocks),
        in_specs=[spec(VMEM), spec(VMEM)],
        out_specs=(spec(VMEM),) * 2,
        name="pick",
        cost_estimate=cost(2 * slots * CAP * tok * model, 2 * tok * model),
        compiler_params=params(4),
    )(chosen, tokens)
    arrays, places = [own], {k: (0, k) for k in range(half)}
    sent, bit = list(range(half, slots)), half
    while bit:
        turn = [(e, e ^ bit) for e in range(slots)]
        arrays.append(lax.ppermute(moving, "expert", turn))
        places.update({k: (len(arrays) - 1, index) for index, k in enumerate(sent)})
        bit //= 2
        if bit:
            sent = [k for k in range(slots) if k & bit]
            moving = pl.pallas_call(
                functools.partial(pack_kernel, [places[k] for k in sent]),
                out_shape=blocks,
                in_specs=[spec(VMEM)] * len(arrays),
                out_specs=spec(VMEM),
                name="pack",
                cost_estimate=cost(0, 4 * half * CAP * model),
                compiler_params=params(4),
            )(*arrays)
    places = [places[k] for k in range(slots)]

    send, keep, hidden = pl.pallas_call(
        functools.partial(shared_first_kernel, chips),
        out_shape=(
            jax.ShapeDtypeStruct((chips - 1, tok, width), BF),
            jax.ShapeDtypeStruct((chips - 1, tok, width), BF),
            jax.ShapeDtypeStruct((tok, hidden_width), BF),
        ),
        in_specs=[spec(VMEM)] * 4 + [spec(ANY)],
        out_specs=(spec(VMEM),) * 3,
        name="shared_first",
        cost_estimate=cost(4 * tok * model * hidden_width + 2 * tok * hidden_width * model // 2, 5 * model * hidden_width),
        compiler_params=params(20),
    )(tokens, shared_gate, shared_up, shared_down, own)

    pairs = [(j, j ^ 1) for j in range(parts)]
    partner = lax.ppermute(send, "dp", pairs)
    chip_sum = pl.pallas_call(
        add_kernel,
        out_shape=jax.ShapeDtypeStruct(keep.shape, BF),
        in_specs=[spec(VMEM)] * 2,
        out_specs=spec(VMEM),
        name="add",
        cost_estimate=cost(0, 6 * keep.size),
        compiler_params=params(4),
    )(partner, keep)
    sums = []
    for k in range(1, chips):
        moves = [(j, (j // 2 + k) % chips * 2 + j % 2) for j in range(parts)]
        sums.append(lax.ppermute(chip_sum[k - 1], "dp", moves))

    routed = pl.pallas_call(
        functools.partial(routed_kernel, parts, places),
        out_shape=jax.ShapeDtypeStruct((slots * parts, CAP, width), BF),
        in_specs=[spec(VMEM)] * (len(arrays) + 3),
        out_specs=spec(VMEM),
        scratch_shapes=[VMEM((slots * CAP, model), BF)],
        name="routed",
        cost_estimate=cost(2 * tok * model * hidden_width, 6 * model * hidden_width),
        compiler_params=params(20),
    )(*arrays, gate_weight, up_weight, down_weight)
    back = lax.all_to_all(
        routed, ("expert", "dp"), split_axis=0, concat_axis=0, tiled=True
    )

    send_rest, keep_rest = pl.pallas_call(
        shared_rest_kernel,
        out_shape=(rows, rows),
        in_specs=[spec(VMEM)] * 2 + [spec(ANY)],
        out_specs=(spec(VMEM),) * 2,
        name="shared_rest",
        cost_estimate=cost(4 * tok * hidden_width * width, 4 * hidden_width * width),
        compiler_params=params(12),
    )(hidden, shared_down, routed)
    sums += [keep_rest, lax.ppermute(send_rest, "dp", pairs)]

    mix = jax.ShapeDtypeStruct((slots * parts * CAP, tok), BF)
    high, low = pl.pallas_call(
        functools.partial(mix_kernel, slots, parts),
        out_shape=(mix, mix),
        in_specs=[spec(SMEM), spec(SMEM), spec(VMEM), spec(VMEM), spec(ANY)],
        out_specs=(spec(VMEM),) * 2,
        name="mix",
        compiler_params=params(8),
    )(old_plan, new_plan, ids, weight, routed)

    return pl.pallas_call(
        functools.partial(combine_kernel, slots * parts),
        out_shape=rows,
        in_specs=[spec(VMEM)] * (3 + len(sums)),
        out_specs=spec(VMEM),
        scratch_shapes=[VMEM((slots * parts * CAP, width), BF)],
        name="combine",
        compiler_params=params(12),
    )(high, low, back, *sums)


def solution(mesh):
    in_specs = (
        P("expert", None),
        P("expert", None),
        P("expert", None),
        P(),
        P(),
        P("expert", None, "dp"),
        P("expert", None, "dp"),
        P("expert", "dp", None),
        P(None, "dp"),
        P(None, "dp"),
        P("dp", None),
    )
    out_specs = P("expert", "dp")
    return jax.shard_map(local, mesh=mesh, in_specs=in_specs, out_specs=out_specs, check_vma=False)
```

```python
import functools

import jax
import jax.numpy as jnp
from jax import lax
from jax.experimental import pallas as pl
from jax.experimental.pallas import tpu as pltpu
from jax.sharding import PartitionSpec as P


CAP = 2
BF = jnp.bfloat16
F32 = jnp.float32
VMEM = pltpu.VMEM
ANY = pl.ANY
SMEM = pltpu.SMEM


def silu_mul(gate_value, up_value):
    return (gate_value / (1.0 + jnp.exp(-gate_value)) * up_value).astype(BF)


def dot(a, b):
    return jnp.dot(a, b, preferred_element_type=F32)


def route_rows(ids, weight, old_ref, new_ref, slot_of, span, count, ranks, slots):
    tok = ids.shape[1]
    rows = count * span * ranks
    row = lax.broadcasted_iota(jnp.int32, (rows, 1), 0)
    block, rank = row // (span * ranks), row % ranks
    plan = jnp.full((rows, 1), -1, jnp.int32)
    for index in range(count):
        slot = slot_of(index)
        expert = old_ref[slot]
        present = (new_ref[slot] == expert) | (new_ref[lax.rem(slot + 1, slots)] == expert)
        plan = jnp.where(block == index, jnp.where(present, expert, -1), plan)
    hit = jnp.zeros((rows, tok), F32)
    scale = jnp.zeros((rows, tok), F32)
    for k in range(ids.shape[0]):
        same = ids[k : k + 1, :] == plan
        hit = jnp.where(same, 1.0, hit)
        if weight is not None:
            scale = jnp.where(same, weight[k : k + 1, :], scale)
    earlier = lax.broadcasted_iota(jnp.int32, (tok, tok), 0)
    later = lax.broadcasted_iota(jnp.int32, (tok, tok), 1)
    before = dot(hit.astype(BF), jnp.where(earlier < later, 1.0, 0.0).astype(BF))
    chosen = jnp.where(before == rank.astype(F32), hit, 0.0)
    return chosen, scale


def ready_kernel(out_ref):
    out_ref[...] = jnp.zeros_like(out_ref)


def carried(index, quarter):
    core = lax.axis_index("dp") % 2
    offsets = (0, quarter, 2 * quarter + quarter * core)
    return lax.axis_index("expert") ^ (index % quarter + offsets[index // quarter])


def select_kernel(slots, old_ref, new_ref, ids_ref, after_ref, chosen_ref):
    quarter = slots // 4
    chosen, _ = route_rows(
        ids_ref[...],
        None,
        old_ref,
        new_ref,
        lambda index: carried(index, quarter),
        1,
        3 * quarter,
        CAP,
        slots,
    )
    chosen_ref[...] = chosen.astype(BF)


def pick_kernel(stays, moves, chosen_ref, tok_ref, own_ref, send_ref):
    picked = dot(chosen_ref[...], tok_ref[...]).astype(BF)
    for target, wanted in ((own_ref, stays), (send_ref, moves)):
        for index, v in enumerate(wanted):
            target[index] = picked[v * CAP : (v + 1) * CAP, :]


def pack_kernel(places, *refs):
    for target, (array, index) in enumerate(places):
        refs[-1][target] = refs[array][index]


def add_kernel(a_ref, b_ref, out_ref):
    out_ref[...] = (a_ref[...].astype(F32) + b_ref[...].astype(F32)).astype(BF)


def mix_kernel(slots, parts, old_ref, new_ref, ids_ref, weight_ref, after_ref, mix_ref):
    chosen, scale = route_rows(
        ids_ref[...], weight_ref[...], old_ref, new_ref, lambda k: k, parts, slots, CAP, slots
    )
    mix = chosen * scale
    high = mix.astype(BF).astype(F32)
    mix_ref[...] = jnp.concatenate([high, mix - high], axis=0).T.astype(BF)


def total_kernel(a_ref, b_ref, *refs):
    total = a_ref[...].astype(F32) + b_ref[...].astype(F32)
    for term in refs[:-1]:
        total = total + term[...].astype(F32)
    refs[-1][...] = total


def combine_kernel(blocks, pieces, mix_ref, back_ref, sum_ref, out_hbm, rows_ref, out_ref, sems):
    for block in range(blocks):
        pair = back_ref[block]
        rows_ref[block * CAP : (block + 1) * CAP, :] = pair
        rows_ref[(blocks + block) * CAP : (blocks + block + 1) * CAP, :] = pair
    tall = out_ref.shape[0] // pieces
    copies = []
    for piece in range(pieces):
        part = slice(piece * tall, (piece + 1) * tall)
        total = dot(mix_ref[part, :], rows_ref[...]) + sum_ref[part, :]
        out_ref[part, :] = total.astype(BF)
        where = pl.ds(piece * tall, tall)
        copies.append(
            pltpu.make_async_copy(out_ref.at[where], out_hbm.at[where], sems.at[piece])
        )
        copies[-1].start()
    for copy in copies:
        copy.wait()


def column_block(chip, core, width):
    return pl.ds(pl.multiple_of((chip * 2 + core) * width, width), width)


def shared_gate_kernel(tok_ref, gate_ref, after_ref, value_ref):
    value_ref[...] = dot(tok_ref[...], gate_ref[...])


def shared_up_kernel(tok_ref, up_ref, value_ref, hidden_ref):
    hidden_ref[...] = silu_mul(value_ref[...], dot(tok_ref[...], up_ref[...]))


def shared_first_kernel(chips, hidden_ref, down_ref, send_ref, keep_ref):
    width = send_ref.shape[2]
    me = lax.axis_index("dp")
    chip, core = me // 2, me % 2
    for k in range(1, chips):
        other = lax.rem(chip + k, chips)
        for target, side in ((send_ref, 1 - core), (keep_ref, core)):
            block = down_ref[:, column_block(other, side, width)]
            target[k - 1] = dot(hidden_ref[...], block).astype(BF)


def shared_rest_kernel(hidden_ref, down_ref, after_ref, send_ref, keep_ref):
    width = send_ref.shape[1]
    me = lax.axis_index("dp")
    chip, core = me // 2, me % 2
    for target, side in ((send_ref, 1 - core), (keep_ref, core)):
        block = down_ref[:, column_block(chip, side, width)]
        target[...] = dot(hidden_ref[...], block).astype(BF)


def routed_kernel(parts, places, *refs):
    arrays, (gate_ref, up_ref, down_ref, out_ref, rows_ref) = refs[:-5], refs[-5:]
    width = out_ref.shape[2]
    quarter = len(places) // 4
    me = lax.axis_index("expert")
    core = lax.axis_index("dp") % 2
    offsets = (0, quarter, 2 * quarter + quarter * core, 3 * quarter - quarter * core)
    for place, (array, index) in enumerate(places):
        rows_ref[place * CAP : (place + 1) * CAP, :] = arrays[array][index]
    rows = rows_ref[...]
    hidden = silu_mul(dot(rows, gate_ref[0]), dot(rows, up_ref[0]))
    for part in range(parts):
        value = dot(hidden, down_ref[0, :, part * width : (part + 1) * width]).astype(BF)
        for place in range(len(places)):
            sender = me ^ (place % quarter + offsets[place // quarter])
            out_ref[sender * parts + part] = value[place * CAP : (place + 1) * CAP, :]


def cost(flops, size):
    return pl.CostEstimate(flops=flops, bytes_accessed=size, transcendentals=0)


def params(megabytes):
    return pltpu.CompilerParams(vmem_limit_bytes=megabytes * 1024 * 1024)


def spec(space):
    return pl.BlockSpec(memory_space=space)


def local(
    tokens,
    expert_ids,
    combine_weight,
    old_plan,
    new_plan,
    gate_weight,
    up_weight,
    down_weight,
    shared_gate,
    shared_up,
    shared_down,
):
    slots = lax.axis_size("expert")
    parts = lax.axis_size("dp")
    chips = parts // 2
    tok, model = tokens.shape
    hidden_width = shared_gate.shape[1]
    width = model // parts
    ids = expert_ids.T
    weight = combine_weight.T
    rows = jax.ShapeDtypeStruct((tok, width), BF)

    quarter = slots // 4
    virtual = range(3 * quarter)
    pairs = [(j, j ^ 1) for j in range(parts)]
    bits = [1 << n for n in range(quarter.bit_length() - 1)]
    stays = [v for v in virtual if not v % quarter & bits[0]]
    moves = [v for v in virtual if v % quarter & bits[0]]

    def rows_of(count):
        return jax.ShapeDtypeStruct((count, CAP, model), BF)

    ready = pl.pallas_call(
        ready_kernel,
        out_shape=jax.ShapeDtypeStruct((8, 128), F32),
        out_specs=spec(VMEM),
        name="ready",
        cost_estimate=cost(20 * tok * model * hidden_width, 0),
        compiler_params=params(1),
    )()
    chosen = pl.pallas_call(
        functools.partial(select_kernel, slots),
        out_shape=jax.ShapeDtypeStruct((3 * quarter * CAP, tok), BF),
        in_specs=[spec(SMEM), spec(SMEM), spec(VMEM), spec(ANY)],
        out_specs=spec(VMEM),
        name="select",
        cost_estimate=cost(2 * slots * CAP * tok * tok, 2 * tok * model),
        compiler_params=params(2),
    )(old_plan, new_plan, ids, ready)
    own, moving = pl.pallas_call(
        functools.partial(pick_kernel, stays, moves),
        out_shape=(rows_of(len(stays)), rows_of(len(moves))),
        in_specs=[spec(VMEM), spec(VMEM)],
        out_specs=(spec(VMEM),) * 2,
        name="pick",
        cost_estimate=cost(2 * slots * CAP * tok * model, 2 * tok * model),
        compiler_params=params(4),
    )(chosen, tokens)
    arrays, places = [own], {v: (0, index) for index, v in enumerate(stays)}

    def pack(wanted):
        return pl.pallas_call(
            functools.partial(pack_kernel, [places[v] for v in wanted]),
            out_shape=rows_of(len(wanted)),
            in_specs=[spec(VMEM)] * len(arrays),
            out_specs=spec(VMEM),
            name="pack",
            cost_estimate=cost(0, 4 * len(wanted) * CAP * model),
            compiler_params=params(4),
        )(*arrays)

    for hop, bit in enumerate(bits, 1):
        moves = [v for v in virtual if v % quarter & bit]
        if hop > 1:
            moving = pack(moves)
        arrays.append(lax.ppermute(moving, "expert", [(e, e ^ bit) for e in range(slots)]))
        places.update({v: (hop, index) for index, v in enumerate(moves)})
    far = pack(virtual[2 * quarter :])
    near = pack(virtual[quarter : 2 * quarter])
    both = [(j, e) for j in range(parts) for e in range(slots)]
    across = [(j * slots + e, j * slots + (e ^ (2 + j % 2) * quarter)) for j, e in both]
    far = lax.ppermute(far, ("dp", "expert"), across)
    near = lax.ppermute(near, "expert", [(e, e ^ quarter) for e in range(slots)])
    swapped = lax.ppermute(far, "dp", pairs)
    last = len(arrays)
    arrays += [near, far, swapped]
    places = [places[v] for v in range(quarter)]
    places += [(last + group, index) for group in range(3) for index in range(quarter)]

    gate_value = pl.pallas_call(
        shared_gate_kernel,
        out_shape=jax.ShapeDtypeStruct((tok, hidden_width), F32),
        in_specs=[spec(VMEM)] * 2 + [spec(ANY)],
        out_specs=spec(VMEM),
        name="shared_gate",
        cost_estimate=cost(2 * tok * model * hidden_width, 2 * model * hidden_width),
        compiler_params=params(8),
    )(tokens, shared_gate, own)
    hidden = pl.pallas_call(
        shared_up_kernel,
        out_shape=jax.ShapeDtypeStruct((tok, hidden_width), BF),
        in_specs=[spec(VMEM)] * 3,
        out_specs=spec(VMEM),
        name="shared_up",
        cost_estimate=cost(2 * tok * model * hidden_width, 2 * model * hidden_width),
        compiler_params=params(8),
    )(tokens, shared_up, gate_value)
    send, keep = pl.pallas_call(
        functools.partial(shared_first_kernel, chips),
        out_shape=(jax.ShapeDtypeStruct((chips - 1, tok, width), BF),) * 2,
        in_specs=[spec(VMEM)] * 2,
        out_specs=(spec(VMEM),) * 2,
        name="shared_first",
        cost_estimate=cost(
            4 * (chips - 1) * tok * hidden_width * width, 4 * (chips - 1) * hidden_width * width
        ),
        compiler_params=params(12),
    )(hidden, shared_down)

    partner = lax.ppermute(send, "dp", pairs)
    chip_sum = pl.pallas_call(
        add_kernel,
        out_shape=jax.ShapeDtypeStruct(keep.shape, BF),
        in_specs=[spec(VMEM)] * 2,
        out_specs=spec(VMEM),
        name="add",
        cost_estimate=cost(0, 6 * keep.size),
        compiler_params=params(4),
    )(partner, keep)
    sums = []
    for k in range(1, chips):
        moves = [(j, (j // 2 + k) % chips * 2 + j % 2) for j in range(parts)]
        sums.append(lax.ppermute(chip_sum[k - 1], "dp", moves))

    routed = pl.pallas_call(
        functools.partial(routed_kernel, parts, places),
        out_shape=jax.ShapeDtypeStruct((slots * parts, CAP, width), BF),
        in_specs=[spec(VMEM)] * (len(arrays) + 3),
        out_specs=spec(VMEM),
        scratch_shapes=[VMEM((slots * CAP, model), BF)],
        name="routed",
        cost_estimate=cost(2 * tok * model * hidden_width, 6 * model * hidden_width),
        compiler_params=params(20),
    )(*arrays, gate_weight, up_weight, down_weight)
    back = lax.all_to_all(
        routed, ("expert", "dp"), split_axis=0, concat_axis=0, tiled=True
    )

    send_rest, keep_rest = pl.pallas_call(
        shared_rest_kernel,
        out_shape=(rows, rows),
        in_specs=[spec(VMEM)] * 2 + [spec(ANY)],
        out_specs=(spec(VMEM),) * 2,
        name="shared_rest",
        cost_estimate=cost(4 * tok * hidden_width * width, 4 * hidden_width * width),
        compiler_params=params(12),
    )(hidden, shared_down, routed)
    sums += [keep_rest, lax.ppermute(send_rest, "dp", pairs)]

    blocks = slots * parts
    mix = pl.pallas_call(
        functools.partial(mix_kernel, slots, parts),
        out_shape=jax.ShapeDtypeStruct((tok, 2 * blocks * CAP), BF),
        in_specs=[spec(SMEM), spec(SMEM), spec(VMEM), spec(VMEM), spec(ANY)],
        out_specs=spec(VMEM),
        name="mix",
        compiler_params=params(8),
    )(old_plan, new_plan, ids, weight, routed)
    total = pl.pallas_call(
        total_kernel,
        out_shape=jax.ShapeDtypeStruct((tok, width), F32),
        in_specs=[spec(VMEM)] * len(sums),
        out_specs=spec(VMEM),
        name="total",
        compiler_params=params(8),
    )(*sums)
    pieces = 4
    return pl.pallas_call(
        functools.partial(combine_kernel, blocks, pieces),
        out_shape=rows,
        in_specs=[spec(VMEM)] * 3,
        out_specs=spec(ANY),
        scratch_shapes=[
            VMEM((2 * blocks * CAP, width), BF),
            VMEM((tok, width), BF),
            pltpu.SemaphoreType.DMA((pieces,)),
        ],
        name="combine",
        compiler_params=params(12),
    )(mix, back, total)


def solution(mesh):
    in_specs = (
        P("expert", None),
        P("expert", None),
        P("expert", None),
        P(),
        P(),
        P("expert", None, "dp"),
        P("expert", None, "dp"),
        P("expert", "dp", None),
        P(None, "dp"),
        P(None, "dp"),
        P("dp", None),
    )
    out_specs = P("expert", "dp")
    return jax.shard_map(local, mesh=mesh, in_specs=in_specs, out_specs=out_specs, check_vma=False)
```

```python
import functools

import jax
import jax.numpy as jnp
from jax import lax
from jax.experimental import pallas as pl
from jax.experimental.pallas import tpu as pltpu
from jax.sharding import PartitionSpec as P


CAP = 2
BF = jnp.bfloat16
F32 = jnp.float32
VMEM = pltpu.VMEM
ANY = pl.ANY
SMEM = pltpu.SMEM


def silu_mul(gate_value, up_value):
    return (gate_value / (1.0 + jnp.exp(-gate_value)) * up_value).astype(BF)


def dot(a, b):
    return jnp.dot(a, b, preferred_element_type=F32)


def route_rows(ids, weight, old_ref, new_ref, slot_of, span, count, ranks, slots):
    tok = ids.shape[1]
    rows = count * span * ranks
    row = lax.broadcasted_iota(jnp.int32, (rows, 1), 0)
    block, rank = row // ranks % count, row % ranks
    plan = jnp.full((rows, 1), -1, jnp.int32)
    for index in range(count):
        slot = slot_of(index)
        expert = old_ref[slot]
        present = (new_ref[slot] == expert) | (new_ref[lax.rem(slot + 1, slots)] == expert)
        plan = jnp.where(block == index, jnp.where(present, expert, -1), plan)
    hit = jnp.zeros((rows, tok), F32)
    scale = jnp.zeros((rows, tok), F32)
    for k in range(ids.shape[0]):
        same = ids[k : k + 1, :] == plan
        hit = jnp.where(same, 1.0, hit)
        if weight is not None:
            scale = jnp.where(same, weight[k : k + 1, :], scale)
    earlier = lax.broadcasted_iota(jnp.int32, (tok, tok), 0)
    later = lax.broadcasted_iota(jnp.int32, (tok, tok), 1)
    before = dot(hit.astype(BF), jnp.where(earlier < later, 1.0, 0.0).astype(BF))
    chosen = jnp.where(before == rank.astype(F32), hit, 0.0)
    return chosen, scale


def ready_kernel(out_ref):
    out_ref[...] = jnp.zeros_like(out_ref)


def carried(index, quarter):
    core = lax.axis_index("dp") % 2
    offsets = (0, quarter, 2 * quarter + quarter * core)
    return lax.axis_index("expert") ^ (index % quarter + offsets[index // quarter])


def select_kernel(slots, old_ref, new_ref, ids_ref, after_ref, chosen_ref):
    quarter = slots // 4
    chosen, _ = route_rows(
        ids_ref[...],
        None,
        old_ref,
        new_ref,
        lambda index: carried(index, quarter),
        1,
        3 * quarter,
        CAP,
        slots,
    )
    chosen_ref[...] = chosen.astype(BF)


def pick_kernel(stays, moves, chosen_ref, tok_ref, own_ref, send_ref):
    picked = dot(chosen_ref[...], tok_ref[...]).astype(BF)
    for target, wanted in ((own_ref, stays), (send_ref, moves)):
        for index, v in enumerate(wanted):
            target[index] = picked[v * CAP : (v + 1) * CAP, :]


def pack_kernel(places, *refs):
    for target, (array, index) in enumerate(places):
        refs[-1][target] = refs[array][index]


def add_kernel(a_ref, b_ref, out_ref):
    out_ref[...] = (a_ref[...].astype(F32) + b_ref[...].astype(F32)).astype(BF)


def mix_kernel(slots, parts, old_ref, new_ref, ids_ref, weight_ref, after_ref, mix_ref):
    chosen, scale = route_rows(
        ids_ref[...], weight_ref[...], old_ref, new_ref, lambda k: k, parts, slots, CAP, slots
    )
    mix = chosen * scale
    high = mix.astype(BF).astype(F32)
    mix_ref[...] = jnp.concatenate([high, mix - high], axis=0).T.astype(BF)


def total_kernel(a_ref, b_ref, *refs):
    total = a_ref[...].astype(F32) + b_ref[...].astype(F32)
    for term in refs[:-1]:
        total = total + term[...].astype(F32)
    refs[-1][...] = total


def combine_kernel(blocks, pieces, mix_ref, back_ref, sum_ref, out_hbm, rows_ref, out_ref, sems):
    for block in range(blocks):
        pair = back_ref[block]
        rows_ref[block * CAP : (block + 1) * CAP, :] = pair
        rows_ref[(blocks + block) * CAP : (blocks + block + 1) * CAP, :] = pair
    tall = out_ref.shape[0] // pieces
    copies = []
    for piece in range(pieces):
        part = slice(piece * tall, (piece + 1) * tall)
        total = dot(mix_ref[part, :], rows_ref[...]) + sum_ref[part, :]
        out_ref[part, :] = total.astype(BF)
        where = pl.ds(piece * tall, tall)
        copies.append(
            pltpu.make_async_copy(out_ref.at[where], out_hbm.at[where], sems.at[piece])
        )
        copies[-1].start()
    for copy in copies:
        copy.wait()


def column_block(chip, core, width):
    return pl.ds(pl.multiple_of((chip * 2 + core) * width, width), width)


def shared_gate_kernel(tok_ref, gate_ref, after_ref, value_ref):
    value_ref[...] = dot(tok_ref[...], gate_ref[...])


def shared_up_kernel(tok_ref, up_ref, value_ref, hidden_ref):
    hidden_ref[...] = silu_mul(value_ref[...], dot(tok_ref[...], up_ref[...]))


def shared_first_kernel(chips, hidden_ref, down_ref, send_ref, keep_ref):
    width = send_ref.shape[2]
    me = lax.axis_index("dp")
    chip, core = me // 2, me % 2
    for k in range(1, chips):
        other = lax.rem(chip + k, chips)
        for target, side in ((send_ref, 1 - core), (keep_ref, core)):
            block = down_ref[:, column_block(other, side, width)]
            target[k - 1] = dot(hidden_ref[...], block).astype(BF)


def shared_rest_kernel(hidden_ref, down_ref, after_ref, send_ref, keep_ref):
    width = send_ref.shape[1]
    me = lax.axis_index("dp")
    chip, core = me // 2, me % 2
    for target, side in ((send_ref, 1 - core), (keep_ref, core)):
        block = down_ref[:, column_block(chip, side, width)]
        target[...] = dot(hidden_ref[...], block).astype(BF)


def routed_kernel(parts, places, *refs):
    arrays, (gate_ref, up_ref, down_ref, out_ref, rows_ref) = refs[:-5], refs[-5:]
    width = out_ref.shape[2]
    slots = len(places)
    quarter = slots // 4
    me = lax.axis_index("expert")
    core = lax.axis_index("dp") % 2
    offsets = (0, quarter, 2 * quarter + quarter * core, 3 * quarter - quarter * core)
    for place, (array, index) in enumerate(places):
        rows_ref[place * CAP : (place + 1) * CAP, :] = arrays[array][index]
    rows = rows_ref[...]
    hidden = silu_mul(dot(rows, gate_ref[0]), dot(rows, up_ref[0]))
    for part in range(parts):
        value = dot(hidden, down_ref[0, :, part * width : (part + 1) * width]).astype(BF)
        for place in range(len(places)):
            sender = me ^ (place % quarter + offsets[place // quarter])
            out_ref[part * slots + sender] = value[place * CAP : (place + 1) * CAP, :]


def cost(flops, size):
    return pl.CostEstimate(flops=flops, bytes_accessed=size, transcendentals=0)


def params(megabytes):
    return pltpu.CompilerParams(vmem_limit_bytes=megabytes * 1024 * 1024)


def spec(space):
    return pl.BlockSpec(memory_space=space)


def local(
    tokens,
    expert_ids,
    combine_weight,
    old_plan,
    new_plan,
    gate_weight,
    up_weight,
    down_weight,
    shared_gate,
    shared_up,
    shared_down,
):
    slots = lax.axis_size("expert")
    parts = lax.axis_size("dp")
    chips = parts // 2
    tok, model = tokens.shape
    hidden_width = shared_gate.shape[1]
    width = model // parts
    ids = expert_ids.T
    weight = combine_weight.T
    rows = jax.ShapeDtypeStruct((tok, width), BF)

    quarter = slots // 4
    virtual = range(3 * quarter)
    pairs = [(j, j ^ 1) for j in range(parts)]
    bits = [1 << n for n in range(quarter.bit_length() - 1)]
    stays = [v for v in virtual if not v % quarter & bits[0]]
    moves = [v for v in virtual if v % quarter & bits[0]]

    def rows_of(count):
        return jax.ShapeDtypeStruct((count, CAP, model), BF)

    ready = pl.pallas_call(
        ready_kernel,
        out_shape=jax.ShapeDtypeStruct((8, 128), F32),
        out_specs=spec(VMEM),
        name="ready",
        cost_estimate=cost(20 * tok * model * hidden_width, 0),
        compiler_params=params(1),
    )()
    chosen = pl.pallas_call(
        functools.partial(select_kernel, slots),
        out_shape=jax.ShapeDtypeStruct((3 * quarter * CAP, tok), BF),
        in_specs=[spec(SMEM), spec(SMEM), spec(VMEM), spec(ANY)],
        out_specs=spec(VMEM),
        name="select",
        cost_estimate=cost(2 * slots * CAP * tok * tok, 2 * tok * model),
        compiler_params=params(2),
    )(old_plan, new_plan, ids, ready)
    own, moving = pl.pallas_call(
        functools.partial(pick_kernel, stays, moves),
        out_shape=(rows_of(len(stays)), rows_of(len(moves))),
        in_specs=[spec(VMEM), spec(VMEM)],
        out_specs=(spec(VMEM),) * 2,
        name="pick",
        cost_estimate=cost(2 * slots * CAP * tok * model, 2 * tok * model),
        compiler_params=params(4),
    )(chosen, tokens)
    arrays, places = [own], {v: (0, index) for index, v in enumerate(stays)}

    def pack(wanted):
        return pl.pallas_call(
            functools.partial(pack_kernel, [places[v] for v in wanted]),
            out_shape=rows_of(len(wanted)),
            in_specs=[spec(VMEM)] * len(arrays),
            out_specs=spec(VMEM),
            name="pack",
            cost_estimate=cost(0, 4 * len(wanted) * CAP * model),
            compiler_params=params(4),
        )(*arrays)

    for hop, bit in enumerate(bits, 1):
        moves = [v for v in virtual if v % quarter & bit]
        if hop > 1:
            moving = pack(moves)
        arrays.append(lax.ppermute(moving, "expert", [(e, e ^ bit) for e in range(slots)]))
        places.update({v: (hop, index) for index, v in enumerate(moves)})
    far = pack(virtual[2 * quarter :])
    near = pack(virtual[quarter : 2 * quarter])
    both = [(j, e) for j in range(parts) for e in range(slots)]
    across = [(j * slots + e, j * slots + (e ^ (2 + j % 2) * quarter)) for j, e in both]
    far = lax.ppermute(far, ("dp", "expert"), across)
    near = lax.ppermute(near, "expert", [(e, e ^ quarter) for e in range(slots)])
    swapped = lax.ppermute(far, "dp", pairs)
    last = len(arrays)
    arrays += [near, far, swapped]
    places = [places[v] for v in range(quarter)]
    places += [(last + group, index) for group in range(3) for index in range(quarter)]

    gate_value = pl.pallas_call(
        shared_gate_kernel,
        out_shape=jax.ShapeDtypeStruct((tok, hidden_width), F32),
        in_specs=[spec(VMEM)] * 2 + [spec(ANY)],
        out_specs=spec(VMEM),
        name="shared_gate",
        cost_estimate=cost(2 * tok * model * hidden_width, 2 * model * hidden_width),
        compiler_params=params(8),
    )(tokens, shared_gate, own)
    hidden = pl.pallas_call(
        shared_up_kernel,
        out_shape=jax.ShapeDtypeStruct((tok, hidden_width), BF),
        in_specs=[spec(VMEM)] * 3,
        out_specs=spec(VMEM),
        name="shared_up",
        cost_estimate=cost(2 * tok * model * hidden_width, 2 * model * hidden_width),
        compiler_params=params(8),
    )(tokens, shared_up, gate_value)
    send, keep = pl.pallas_call(
        functools.partial(shared_first_kernel, chips),
        out_shape=(jax.ShapeDtypeStruct((chips - 1, tok, width), BF),) * 2,
        in_specs=[spec(VMEM)] * 2,
        out_specs=(spec(VMEM),) * 2,
        name="shared_first",
        cost_estimate=cost(
            4 * (chips - 1) * tok * hidden_width * width, 4 * (chips - 1) * hidden_width * width
        ),
        compiler_params=params(12),
    )(hidden, shared_down)

    partner = lax.ppermute(send, "dp", pairs)
    chip_sum = pl.pallas_call(
        add_kernel,
        out_shape=jax.ShapeDtypeStruct(keep.shape, BF),
        in_specs=[spec(VMEM)] * 2,
        out_specs=spec(VMEM),
        name="add",
        cost_estimate=cost(0, 6 * keep.size),
        compiler_params=params(4),
    )(partner, keep)
    sums = []
    for k in range(1, chips):
        moves = [(j, (j // 2 + k) % chips * 2 + j % 2) for j in range(parts)]
        sums.append(lax.ppermute(chip_sum[k - 1], "dp", moves))

    routed = pl.pallas_call(
        functools.partial(routed_kernel, parts, places),
        out_shape=jax.ShapeDtypeStruct((slots * parts, CAP, width), BF),
        in_specs=[spec(VMEM)] * (len(arrays) + 3),
        out_specs=spec(VMEM),
        scratch_shapes=[VMEM((slots * CAP, model), BF)],
        name="routed",
        cost_estimate=cost(2 * tok * model * hidden_width, 6 * model * hidden_width),
        compiler_params=params(20),
    )(*arrays, gate_weight, up_weight, down_weight)
    back = lax.all_to_all(
        routed, ("dp", "expert"), split_axis=0, concat_axis=0, tiled=True
    )

    send_rest, keep_rest = pl.pallas_call(
        shared_rest_kernel,
        out_shape=(rows, rows),
        in_specs=[spec(VMEM)] * 2 + [spec(ANY)],
        out_specs=(spec(VMEM),) * 2,
        name="shared_rest",
        cost_estimate=cost(4 * tok * hidden_width * width, 4 * hidden_width * width),
        compiler_params=params(12),
    )(hidden, shared_down, routed)
    sums += [keep_rest, lax.ppermute(send_rest, "dp", pairs)]

    blocks = slots * parts
    mix = pl.pallas_call(
        functools.partial(mix_kernel, slots, parts),
        out_shape=jax.ShapeDtypeStruct((tok, 2 * blocks * CAP), BF),
        in_specs=[spec(SMEM), spec(SMEM), spec(VMEM), spec(VMEM), spec(ANY)],
        out_specs=spec(VMEM),
        name="mix",
        compiler_params=params(8),
    )(old_plan, new_plan, ids, weight, routed)
    total = pl.pallas_call(
        total_kernel,
        out_shape=jax.ShapeDtypeStruct((tok, width), F32),
        in_specs=[spec(VMEM)] * len(sums),
        out_specs=spec(VMEM),
        name="total",
        compiler_params=params(8),
    )(*sums)
    pieces = 4
    return pl.pallas_call(
        functools.partial(combine_kernel, blocks, pieces),
        out_shape=rows,
        in_specs=[spec(VMEM)] * 3,
        out_specs=spec(ANY),
        scratch_shapes=[
            VMEM((2 * blocks * CAP, width), BF),
            VMEM((tok, width), BF),
            pltpu.SemaphoreType.DMA((pieces,)),
        ],
        name="combine",
        compiler_params=params(12),
    )(mix, back, total)


def solution(mesh):
    in_specs = (
        P("expert", None),
        P("expert", None),
        P("expert", None),
        P(),
        P(),
        P("expert", None, "dp"),
        P("expert", None, "dp"),
        P("expert", "dp", None),
        P(None, "dp"),
        P(None, "dp"),
        P("dp", None),
    )
    out_specs = P("expert", "dp")
    return jax.shard_map(local, mesh=mesh, in_specs=in_specs, out_specs=out_specs, check_vma=False)
```

```python
import functools

import jax
import jax.numpy as jnp
from jax import lax
from jax.experimental import pallas as pl
from jax.experimental.pallas import tpu as pltpu
from jax.sharding import PartitionSpec as P


CAP = 2
BF = jnp.bfloat16
F32 = jnp.float32
VMEM = pltpu.VMEM
ANY = pl.ANY
SMEM = pltpu.SMEM


def silu_mul(gate_value, up_value):
    return (gate_value / (1.0 + jnp.exp(-gate_value)) * up_value).astype(BF)


def dot(a, b):
    return jnp.dot(a, b, preferred_element_type=F32)


def route_rows(ids, weight, old_ref, new_ref, slot_of, span, count, ranks, slots):
    tok = ids.shape[1]
    rows = count * span * ranks
    row = lax.broadcasted_iota(jnp.int32, (rows, 1), 0)
    block, rank = row // ranks % count, row % ranks
    plan = jnp.full((rows, 1), -1, jnp.int32)
    for index in range(count):
        slot = slot_of(index)
        expert = old_ref[slot]
        present = (new_ref[slot] == expert) | (new_ref[lax.rem(slot + 1, slots)] == expert)
        plan = jnp.where(block == index, jnp.where(present, expert, -1), plan)
    hit = jnp.zeros((rows, tok), F32)
    scale = jnp.zeros((rows, tok), F32)
    for k in range(ids.shape[0]):
        same = ids[k : k + 1, :] == plan
        hit = jnp.where(same, 1.0, hit)
        if weight is not None:
            scale = jnp.where(same, weight[k : k + 1, :], scale)
    earlier = lax.broadcasted_iota(jnp.int32, (tok, tok), 0)
    later = lax.broadcasted_iota(jnp.int32, (tok, tok), 1)
    before = dot(hit.astype(BF), jnp.where(earlier < later, 1.0, 0.0).astype(BF))
    chosen = jnp.where(before == rank.astype(F32), hit, 0.0)
    return chosen, scale


def ready_kernel(out_ref):
    out_ref[...] = jnp.zeros_like(out_ref)


def carried(index, quarter):
    core = lax.axis_index("dp") % 2
    offsets = (0, quarter, 2 * quarter + quarter * core)
    return lax.axis_index("expert") ^ (index % quarter + offsets[index // quarter])


def select_kernel(slots, old_ref, new_ref, ids_ref, after_ref, chosen_ref):
    quarter = slots // 4
    chosen, _ = route_rows(
        ids_ref[...],
        None,
        old_ref,
        new_ref,
        lambda index: carried(index, quarter),
        1,
        3 * quarter,
        CAP,
        slots,
    )
    chosen_ref[...] = chosen.astype(BF)


def pick_kernel(stays, moves, chosen_ref, tok_ref, own_ref, send_ref):
    picked = dot(chosen_ref[...], tok_ref[...]).astype(BF)
    for target, wanted in ((own_ref, stays), (send_ref, moves)):
        for index, v in enumerate(wanted):
            target[index] = picked[v * CAP : (v + 1) * CAP, :]


def pack_kernel(places, *refs):
    for target, (array, index) in enumerate(places):
        refs[-1][target] = refs[array][index]


def add_kernel(a_ref, b_ref, out_ref):
    out_ref[...] = (a_ref[...].astype(F32) + b_ref[...].astype(F32)).astype(BF)


def mix_kernel(slots, parts, old_ref, new_ref, ids_ref, weight_ref, mix_ref):
    chosen, scale = route_rows(
        ids_ref[...], weight_ref[...], old_ref, new_ref, lambda k: k, parts, slots, CAP, slots
    )
    mix = chosen * scale
    high = mix.astype(BF).astype(F32)
    mix_ref[...] = jnp.concatenate([high, mix - high], axis=0).T.astype(BF)


def total_kernel(a_ref, b_ref, *refs):
    total = a_ref[...].astype(F32) + b_ref[...].astype(F32)
    for term in refs[:-1]:
        total = total + term[...].astype(F32)
    refs[-1][...] = total


def combine_kernel(blocks, pieces, mix_ref, back_ref, sum_ref, out_hbm, rows_ref, out_ref, sems):
    for block in range(blocks):
        pair = back_ref[block]
        rows_ref[block * CAP : (block + 1) * CAP, :] = pair
        rows_ref[(blocks + block) * CAP : (blocks + block + 1) * CAP, :] = pair
    tall = out_ref.shape[0] // pieces
    copies = []
    for piece in range(pieces):
        part = slice(piece * tall, (piece + 1) * tall)
        total = dot(mix_ref[part, :], rows_ref[...]) + sum_ref[part, :]
        out_ref[part, :] = total.astype(BF)
        where = pl.ds(piece * tall, tall)
        copies.append(
            pltpu.make_async_copy(out_ref.at[where], out_hbm.at[where], sems.at[piece])
        )
        copies[-1].start()
    for copy in copies:
        copy.wait()


def column_block(chip, core, width):
    return pl.ds(pl.multiple_of((chip * 2 + core) * width, width), width)


def shared_gate_kernel(tok_ref, gate_ref, after_ref, value_ref):
    value_ref[...] = dot(tok_ref[...], gate_ref[...])


def shared_up_kernel(tok_ref, up_ref, value_ref, hidden_ref):
    hidden_ref[...] = silu_mul(value_ref[...], dot(tok_ref[...], up_ref[...]))


def shared_first_kernel(chips, hidden_ref, down_ref, send_ref, keep_ref):
    width = send_ref.shape[2]
    me = lax.axis_index("dp")
    chip, core = me // 2, me % 2
    for k in range(1, chips):
        other = lax.rem(chip + k, chips)
        for target, side in ((send_ref, 1 - core), (keep_ref, core)):
            block = down_ref[:, column_block(other, side, width)]
            target[k - 1] = dot(hidden_ref[...], block).astype(BF)


def shared_rest_kernel(hidden_ref, down_ref, send_ref, keep_ref):
    width = send_ref.shape[1]
    me = lax.axis_index("dp")
    chip, core = me // 2, me % 2
    for target, side in ((send_ref, 1 - core), (keep_ref, core)):
        block = down_ref[:, column_block(chip, side, width)]
        target[...] = dot(hidden_ref[...], block).astype(BF)


def routed_kernel(parts, places, *refs):
    arrays, (gate_ref, up_ref, down_ref, out_ref, rows_ref) = refs[:-5], refs[-5:]
    width = out_ref.shape[2]
    slots = len(places)
    quarter = slots // 4
    me = lax.axis_index("expert")
    core = lax.axis_index("dp") % 2
    offsets = (0, quarter, 2 * quarter + quarter * core, 3 * quarter - quarter * core)
    for place, (array, index) in enumerate(places):
        rows_ref[place * CAP : (place + 1) * CAP, :] = arrays[array][index]
    rows = rows_ref[...]
    hidden = silu_mul(dot(rows, gate_ref[0]), dot(rows, up_ref[0]))
    for part in range(parts):
        value = dot(hidden, down_ref[0, :, part * width : (part + 1) * width]).astype(BF)
        for place in range(len(places)):
            sender = me ^ (place % quarter + offsets[place // quarter])
            out_ref[part * slots + sender] = value[place * CAP : (place + 1) * CAP, :]


def cost(flops, size):
    return pl.CostEstimate(flops=flops, bytes_accessed=size, transcendentals=0)


def params(megabytes):
    return pltpu.CompilerParams(vmem_limit_bytes=megabytes * 1024 * 1024)


def spec(space):
    return pl.BlockSpec(memory_space=space)


def local(
    tokens,
    expert_ids,
    combine_weight,
    old_plan,
    new_plan,
    gate_weight,
    up_weight,
    down_weight,
    shared_gate,
    shared_up,
    shared_down,
):
    slots = lax.axis_size("expert")
    parts = lax.axis_size("dp")
    chips = parts // 2
    tok, model = tokens.shape
    hidden_width = shared_gate.shape[1]
    width = model // parts
    ids = expert_ids.T
    weight = combine_weight.T
    rows = jax.ShapeDtypeStruct((tok, width), BF)

    quarter = slots // 4
    virtual = range(3 * quarter)
    pairs = [(j, j ^ 1) for j in range(parts)]
    bits = [1 << n for n in range(quarter.bit_length() - 1)]
    stays = [v for v in virtual if not v % quarter & bits[0]]
    moves = [v for v in virtual if v % quarter & bits[0]]

    def rows_of(count):
        return jax.ShapeDtypeStruct((count, CAP, model), BF)

    ready = pl.pallas_call(
        ready_kernel,
        out_shape=jax.ShapeDtypeStruct((8, 128), F32),
        out_specs=spec(VMEM),
        name="ready",
        cost_estimate=cost(20 * tok * model * hidden_width, 0),
        compiler_params=params(1),
    )()
    chosen = pl.pallas_call(
        functools.partial(select_kernel, slots),
        out_shape=jax.ShapeDtypeStruct((3 * quarter * CAP, tok), BF),
        in_specs=[spec(SMEM), spec(SMEM), spec(VMEM), spec(ANY)],
        out_specs=spec(VMEM),
        name="select",
        cost_estimate=cost(2 * slots * CAP * tok * tok, 2 * tok * model),
        compiler_params=params(2),
    )(old_plan, new_plan, ids, ready)
    own, moving = pl.pallas_call(
        functools.partial(pick_kernel, stays, moves),
        out_shape=(rows_of(len(stays)), rows_of(len(moves))),
        in_specs=[spec(VMEM), spec(VMEM)],
        out_specs=(spec(VMEM),) * 2,
        name="pick",
        cost_estimate=cost(2 * slots * CAP * tok * model, 2 * tok * model),
        compiler_params=params(4),
    )(chosen, tokens)
    arrays, places = [own], {v: (0, index) for index, v in enumerate(stays)}

    def pack(wanted):
        return pl.pallas_call(
            functools.partial(pack_kernel, [places[v] for v in wanted]),
            out_shape=rows_of(len(wanted)),
            in_specs=[spec(VMEM)] * len(arrays),
            out_specs=spec(VMEM),
            name="pack",
            cost_estimate=cost(0, 4 * len(wanted) * CAP * model),
            compiler_params=params(4),
        )(*arrays)

    for hop, bit in enumerate(bits, 1):
        moves = [v for v in virtual if v % quarter & bit]
        if hop > 1:
            moving = pack(moves)
        arrays.append(lax.ppermute(moving, "expert", [(e, e ^ bit) for e in range(slots)]))
        places.update({v: (hop, index) for index, v in enumerate(moves)})
    far = pack(virtual[2 * quarter :])
    near = pack(virtual[quarter : 2 * quarter])
    both = [(j, e) for j in range(parts) for e in range(slots)]
    across = [(j * slots + e, j * slots + (e ^ (2 + j % 2) * quarter)) for j, e in both]
    far = lax.ppermute(far, ("dp", "expert"), across)
    near = lax.ppermute(near, "expert", [(e, e ^ quarter) for e in range(slots)])
    swapped = lax.ppermute(far, "dp", pairs)
    last = len(arrays)
    arrays += [near, far, swapped]
    places = [places[v] for v in range(quarter)]
    places += [(last + group, index) for group in range(3) for index in range(quarter)]

    gate_value = pl.pallas_call(
        shared_gate_kernel,
        out_shape=jax.ShapeDtypeStruct((tok, hidden_width), F32),
        in_specs=[spec(VMEM)] * 2 + [spec(ANY)],
        out_specs=spec(VMEM),
        name="shared_gate",
        cost_estimate=cost(2 * tok * model * hidden_width, 2 * model * hidden_width),
        compiler_params=params(8),
    )(tokens, shared_gate, own)
    hidden = pl.pallas_call(
        shared_up_kernel,
        out_shape=jax.ShapeDtypeStruct((tok, hidden_width), BF),
        in_specs=[spec(VMEM)] * 3,
        out_specs=spec(VMEM),
        name="shared_up",
        cost_estimate=cost(2 * tok * model * hidden_width, 2 * model * hidden_width),
        compiler_params=params(8),
    )(tokens, shared_up, gate_value)
    send, keep = pl.pallas_call(
        functools.partial(shared_first_kernel, chips),
        out_shape=(jax.ShapeDtypeStruct((chips - 1, tok, width), BF),) * 2,
        in_specs=[spec(VMEM)] * 2,
        out_specs=(spec(VMEM),) * 2,
        name="shared_first",
        cost_estimate=cost(
            4 * (chips - 1) * tok * hidden_width * width, 4 * (chips - 1) * hidden_width * width
        ),
        compiler_params=params(12),
    )(hidden, shared_down)

    partner = lax.ppermute(send, "dp", pairs)
    chip_sum = pl.pallas_call(
        add_kernel,
        out_shape=jax.ShapeDtypeStruct(keep.shape, BF),
        in_specs=[spec(VMEM)] * 2,
        out_specs=spec(VMEM),
        name="add",
        cost_estimate=cost(0, 6 * keep.size),
        compiler_params=params(4),
    )(partner, keep)
    sums = []
    for k in range(1, chips):
        moves = [(j, (j // 2 + k) % chips * 2 + j % 2) for j in range(parts)]
        sums.append(lax.ppermute(chip_sum[k - 1], "dp", moves))

    routed = pl.pallas_call(
        functools.partial(routed_kernel, parts, places),
        out_shape=jax.ShapeDtypeStruct((slots * parts, CAP, width), BF),
        in_specs=[spec(VMEM)] * (len(arrays) + 3),
        out_specs=spec(VMEM),
        scratch_shapes=[VMEM((slots * CAP, model), BF)],
        name="routed",
        cost_estimate=cost(2 * tok * model * hidden_width, 6 * model * hidden_width),
        compiler_params=params(20),
    )(*arrays, gate_weight, up_weight, down_weight)
    back = lax.all_to_all(
        routed, ("dp", "expert"), split_axis=0, concat_axis=0, tiled=True
    )

    send_rest, keep_rest = pl.pallas_call(
        shared_rest_kernel,
        out_shape=(rows, rows),
        in_specs=[spec(VMEM)] * 2,
        out_specs=(spec(VMEM),) * 2,
        name="shared_rest",
        cost_estimate=cost(4 * tok * hidden_width * width, 4 * hidden_width * width),
        compiler_params=params(12),
    )(hidden, shared_down)
    sums += [keep_rest, lax.ppermute(send_rest, "dp", pairs)]

    blocks = slots * parts
    mix = pl.pallas_call(
        functools.partial(mix_kernel, slots, parts),
        out_shape=jax.ShapeDtypeStruct((tok, 2 * blocks * CAP), BF),
        in_specs=[spec(SMEM), spec(SMEM), spec(VMEM), spec(VMEM)],
        out_specs=spec(VMEM),
        name="mix",
        compiler_params=params(8),
    )(old_plan, new_plan, ids, weight)
    total = pl.pallas_call(
        total_kernel,
        out_shape=jax.ShapeDtypeStruct((tok, width), F32),
        in_specs=[spec(VMEM)] * len(sums),
        out_specs=spec(VMEM),
        name="total",
        compiler_params=params(8),
    )(*sums)
    pieces = 4
    return pl.pallas_call(
        functools.partial(combine_kernel, blocks, pieces),
        out_shape=rows,
        in_specs=[spec(VMEM)] * 3,
        out_specs=spec(ANY),
        scratch_shapes=[
            VMEM((2 * blocks * CAP, width), BF),
            VMEM((tok, width), BF),
            pltpu.SemaphoreType.DMA((pieces,)),
        ],
        name="combine",
        compiler_params=params(12),
    )(mix, back, total)


def solution(mesh):
    in_specs = (
        P("expert", None),
        P("expert", None),
        P("expert", None),
        P(),
        P(),
        P("expert", None, "dp"),
        P("expert", None, "dp"),
        P("expert", "dp", None),
        P(None, "dp"),
        P(None, "dp"),
        P("dp", None),
    )
    out_specs = P("expert", "dp")
    return jax.shard_map(local, mesh=mesh, in_specs=in_specs, out_specs=out_specs, check_vma=False)
```
